256 devices in a mesh: grp: 8 (over y, core), row: 32 (over z, x).
Axes of the slice: x: 4, y: 4, z: 8, core: 2. Of those that a mesh axis runs over, the one named last changes fastest.
Arguments:
- features: bfloat16 [524288, 256], P(('grp', 'row')), may hold values from -6 to 6
- cotangent: bfloat16 [524288, 256], P(('grp', 'row')), may hold values from -6 to 6
- self_weight: bfloat16 [256, 256], replicated, may hold values from -0.375 to 0.375
- neighbor_weight: bfloat16 [256, 256], replicated, may hold values from -0.375 to 0.375
- tile_values: bfloat16 [256, 64, 128, 128], P(('grp', 'row')), may hold values from 0 to 1
- tile_index: int32 [256, 64, 2], P(('grp', 'row')), may hold values from 0 to 15
- hub_adjacency: bfloat16 [524288, 1024], P(('grp', 'row')), may hold values from 0 to 1
- hub_owner: int32 [8, 8], P('grp'), may hold values from 0 to 31
- send_rows: int32 [256, 8, 64], P(('grp', 'row')), may hold values from 0 to 2047
- cut_adjacency: bfloat16 [524288, 512], P(('grp', 'row')), may hold values from 0 to 1
- degrees: int32 [524288], P(('grp', 'row')), may hold values from 1024 to 2047
Outputs:
- hidden: bfloat16 [524288, 256], P(('grp', 'row'))
- grad_features: bfloat16 [524288, 256], P(('grp', 'row'))
- grad_self: float32 [256, 256], replicated
- grad_neighbor: float32 [256, 256], replicated
The draws below stay inside these ranges and needn't reach their ends.
Inputs may be any that keep to these rules, and one draw needn't show every extreme that they name: `send_rows`: rows may repeat.
All inputs are finite; a program needn't handle non-finite values.
Results may differ from the reference program's by a relative error of at most 0.014.
Values may be sent and summed in bfloat16 or wider, within the bound.
A program may use at most 128 MiB of HBM per device.

```python
import jax
import jax.numpy as jnp
from jax import lax

WIDTH = 256
TILE = 128
TILES_DEV = 16
HUB = 128
SECTIONS = 8
CUT = 64
TILES = 64
NODE_DEV = 2048
NODES = 524288
NEIGHBORS = 2048
N_GRP = 8
N_ROW = 32


def touch_ends(entries, own_key, low, top_value):
    longest = entries.shape.index(max(entries.shape))
    spots = []
    for shift in (0, 1):
        where = [jax.random.randint(jax.random.fold_in(own_key, axis), (), 0, length) for axis, length in enumerate(entries.shape)]
        where[longest] = (where[longest] + shift) % entries.shape[longest]
        spots.append(tuple(where))
    return entries.at[spots[0]].set(low).at[spots[1]].set(top_value)


def block_levels(own_key, extent, cuts, low, high):
    loudness, own = 1.0, jax.random.fold_in(own_key, 6)
    for dim, shards_of in cuts:
        steps = jnp.exp(jax.random.uniform(jax.random.fold_in(own, dim), (shards_of,), jnp.float32, low / len(cuts), high / len(cuts)))
        loudness = loudness * jnp.repeat(steps, extent[dim] // shards_of).reshape([-1 if axis == dim else 1 for axis in range(len(extent))])
    return loudness


def scatter_about(key, shape, spread, most, cuts=(), kind=jnp.bfloat16):
    drawn = jax.random.normal(key, shape, jnp.float32) * spread
    if len(cuts) > 0:
        drawn = block_levels(key, shape, cuts, -0.22, 0.18) * drawn
    return jnp.clip(drawn, min=-most, max=most).astype(kind)


def setup_inputs(seed: int = 0) -> dict:
    key_of = jax.random.split(jax.random.key(seed), 12)
    return {
        "features": scatter_about(key_of[0], (NODES, WIDTH), 1.0, 6.0, ((0, 256),)),
        "cotangent": scatter_about(key_of[1], (NODES, WIDTH), 1.0, 6.0, ((0, 256),)),
        "self_weight": scatter_about(key_of[2], (WIDTH, WIDTH), WIDTH ** -0.5, 0.375),
        "neighbor_weight": scatter_about(key_of[3], (WIDTH, WIDTH), WIDTH ** -0.5, 0.375),
        "tile_values": jnp.clip(1.0 * jax.random.uniform(key_of[4], (N_GRP * N_ROW, TILES, TILE, TILE), jnp.float32) ** block_levels(key_of[4], (N_GRP * N_ROW, TILES, TILE, TILE), ((0, 256),), -0.2, 0.2), 0.0, 1.0).astype(jnp.bfloat16),
        "tile_index": touch_ends(jax.random.randint(key_of[5], (N_GRP * N_ROW, TILES, 2), 0, TILES_DEV), jax.random.fold_in(key_of[5], 1), 0, TILES_DEV - 1).astype(jnp.int32),
        "hub_adjacency": jnp.clip(1.0 * jax.random.uniform(key_of[6], (NODES, SECTIONS * HUB), jnp.float32) ** block_levels(key_of[6], (NODES, SECTIONS * HUB), ((0, 256),), -0.2, 0.2), 0.0, 1.0).astype(jnp.bfloat16),
        "hub_owner": touch_ends(jax.random.randint(key_of[7], (N_GRP, SECTIONS), 0, N_ROW), jax.random.fold_in(key_of[7], 1), 0, N_ROW - 1).astype(jnp.int32),
        "send_rows": touch_ends(jax.random.randint(key_of[8], (N_GRP * N_ROW, N_GRP, CUT), 0, NODE_DEV), jax.random.fold_in(key_of[8], 1), 0, NODE_DEV - 1).astype(jnp.int32),
        "cut_adjacency": jnp.clip(1.0 * jax.random.uniform(key_of[9], (NODES, N_GRP * CUT), jnp.float32) ** block_levels(key_of[9], (NODES, N_GRP * CUT), ((0, 256),), -0.2, 0.2), 0.0, 1.0).astype(jnp.bfloat16),
        "degrees": touch_ends(jax.random.randint(key_of[10], (NODES,), NEIGHBORS // 2, NEIGHBORS), jax.random.fold_in(key_of[10], 1), NEIGHBORS // 2, NEIGHBORS - 1).astype(jnp.int32),
    }


def device_pass(items, self_weight, neighbor_weight):
    features, cotangent, values, index, hub_rows, panels, cut_rows, arrived, degree = items
    tile_total = features.shape[0] // TILE
    width = features.shape[1]
    blocks = features.reshape(tile_total, TILE, width)
    row_select = (index[:, 0][None, :] == jnp.arange(tile_total)[:, None]).astype(jnp.float32)
    col_select = (index[:, 1][None, :] == jnp.arange(tile_total)[:, None]).astype(jnp.float32)
    picked = blocks[index[:, 1]]
    product = jnp.einsum('lab,lbf->laf', values.astype(jnp.float32), picked.astype(jnp.float32), precision=lax.Precision.HIGHEST)
    local_sum = jnp.einsum('nl,laf->naf', row_select, product, precision=lax.Precision.HIGHEST).reshape(-1, width)
    hub_sum = jnp.dot(hub_rows, panels, preferred_element_type=jnp.float32)
    cut_sum = jnp.dot(cut_rows, arrived, preferred_element_type=jnp.float32)
    scaling = lax.rsqrt(degree.astype(jnp.float32))[:, None]
    aggregated = ((local_sum + hub_sum + cut_sum) * scaling).astype(jnp.bfloat16)
    before = jnp.dot(features, self_weight, preferred_element_type=jnp.float32) + jnp.dot(aggregated, neighbor_weight, preferred_element_type=jnp.float32)
    activated, pullback = jax.vjp(jax.nn.gelu, before)
    hidden = activated.astype(jnp.bfloat16)
    grad_before = pullback(cotangent.astype(before.dtype))[0].astype(jnp.bfloat16)
    rows_dims = (((0,), (0,)), ((), ()))
    cols_dims = (((1,), (1,)), ((), ()))
    self_part = lax.dot_general(features, grad_before, rows_dims, preferred_element_type=jnp.float32)
    neighbor_part = lax.dot_general(aggregated, grad_before, rows_dims, preferred_element_type=jnp.float32)
    grad_aggregate = (lax.dot_general(grad_before, neighbor_weight, cols_dims, preferred_element_type=jnp.float32) * scaling).astype(jnp.bfloat16)
    grad_part = lax.dot_general(grad_before, self_weight, cols_dims, preferred_element_type=jnp.float32)
    agg_blocks = grad_aggregate.reshape(tile_total, TILE, width)[index[:, 0]]
    returned = jnp.einsum('lab,laf->lbf', values.astype(jnp.float32), agg_blocks.astype(jnp.float32), precision=lax.Precision.HIGHEST)
    grad_part = grad_part + jnp.einsum('nl,lbf->nbf', col_select, returned, precision=lax.Precision.HIGHEST).reshape(-1, width)
    hub_terms = lax.dot_general(hub_rows, grad_aggregate, rows_dims, preferred_element_type=jnp.float32)
    back_rows = lax.dot_general(cut_rows, grad_aggregate, rows_dims, preferred_element_type=jnp.float32).astype(jnp.bfloat16)
    return (hidden, grad_part, self_part, neighbor_part, hub_terms, back_rows)

def scatter_back(items):
    returned, rows = items
    table = (rows[None, :] == jnp.arange(NODE_DEV)[:, None]).astype(jnp.bfloat16)
    return jnp.dot(table, returned, preferred_element_type=jnp.float32)

def reference(features, cotangent, self_weight, neighbor_weight, tile_values, tile_index, hub_adjacency, hub_owner, send_rows, cut_adjacency, degrees):
    groups = N_GRP
    rows_axis = N_ROW
    blocks_all = groups * rows_axis
    width = WIDTH
    block_feats = features.reshape(blocks_all, NODE_DEV, width)
    block_cots = cotangent.reshape(blocks_all, NODE_DEV, width)
    block_hubs = hub_adjacency.reshape(blocks_all, NODE_DEV, SECTIONS * HUB)
    block_cuts = cut_adjacency.reshape(blocks_all, NODE_DEV, groups * CUT)
    block_degs = degrees.reshape(blocks_all, NODE_DEV)
    heads = block_feats[:, :HUB].reshape(groups, rows_axis, HUB, width)
    panels = heads[jnp.arange(groups)[:, None], hub_owner]
    panels = jnp.broadcast_to(panels.reshape(groups, 1, SECTIONS * HUB, width), (groups, rows_axis, SECTIONS * HUB, width)).reshape(blocks_all, SECTIONS * HUB, width)
    outgoing = jax.vmap(lambda block, rows: block[rows])(block_feats, send_rows)
    arrived = outgoing.reshape(groups, rows_axis, groups, CUT, width).transpose(2, 1, 0, 3, 4).reshape(blocks_all, groups * CUT, width)
    items = (block_feats, block_cots, tile_values, tile_index, block_hubs, panels, block_cuts, arrived, block_degs)
    hidden, grad_part, self_parts, neighbor_parts, hub_terms, back_rows = lax.map(lambda item: device_pass(item, self_weight, neighbor_weight), items)
    grad_self = lax.optimization_barrier(jnp.sum(self_parts, axis=0))
    grad_neighbor = lax.optimization_barrier(jnp.sum(neighbor_parts, axis=0))
    hub_total = hub_terms.reshape(groups, rows_axis, SECTIONS, HUB, width).sum(axis=1)
    owned = (hub_owner[:, :, None] == jnp.arange(rows_axis)[None, None, :]).astype(hub_total.dtype)
    hub_grad = jnp.einsum('gsr,gshf->grhf', owned, hub_total, precision=lax.Precision.HIGHEST).reshape(blocks_all, HUB, width)
    returned = back_rows.reshape(groups, rows_axis, groups, CUT, width).transpose(2, 1, 0, 3, 4).reshape(blocks_all, groups * CUT, width)
    cut_grad = lax.map(scatter_back, (returned, send_rows.reshape(blocks_all, groups * CUT)))
    total = grad_part + cut_grad
    total = total.at[:, :HUB].add(hub_grad)
    return (hidden.reshape(NODES, width), total.astype(jnp.bfloat16).reshape(NODES, width), grad_self, grad_neighbor)
```

```python
import jax
import jax.numpy as jnp
from jax import lax
from jax.experimental import pallas as pl
from jax.experimental.pallas import tpu as pltpu
from jax.sharding import PartitionSpec as P

TILE = 128
HUB = 128
ACROSS = 4
CHUNK = 256
F32 = jnp.float32
BF16 = jnp.bfloat16
VMEM = pl.BlockSpec(memory_space=pltpu.VMEM)
SMEM = pl.BlockSpec(memory_space=pltpu.SMEM)
MESH = pl.DeviceIdType.MESH


def dot(left, right):
    return jnp.dot(left, right, preferred_element_type=F32)


def dot_cols(left, right):
    return lax.dot_general(left, right, (((1,), (1,)), ((), ())), preferred_element_type=F32)


class Place:
    def __init__(self):
        self.row = lax.axis_index("row")
        self.grp = lax.axis_index("grp")
        self.groups = lax.axis_size("grp")
        self.depth = lax.axis_size("row") // ACROSS
        self.x = lax.rem(self.row, ACROSS)
        self.z = lax.div(self.row, ACROSS)

    def along_x(self, shift):
        peer = lax.rem(self.x + shift, ACROSS)
        return peer, {"row": self.z * ACROSS + peer}

    def along_z(self, shift):
        peer = lax.rem(self.z + shift, self.depth)
        return peer, {"row": peer * ACROSS + self.x}

    def along_grp(self, shift):
        peer = lax.rem(self.grp + shift, self.groups)
        return peer, {"grp": peer}

    def greet(self):
        barrier = pltpu.get_barrier_semaphore()
        count = 0
        for peers, size in (
            (self.along_x, ACROSS),
            (self.along_z, self.depth),
            (self.along_grp, self.groups),
        ):
            for shift in range(1, size):
                pl.semaphore_signal(
                    barrier, inc=1, device_id=peers(shift)[1], device_id_type=MESH
                )
                count += 1
        pl.semaphore_wait(barrier, count)


def send_all(peers, size, source, target, sems):
    send, recv = sems
    copies = []
    for shift in range(1, size):
        peer, device = peers(shift)
        copy = pltpu.make_async_remote_copy(
            src_ref=source(peer, shift),
            dst_ref=target(shift),
            send_sem=send.at[shift - 1],
            recv_sem=recv.at[shift - 1],
            device_id=device,
            device_id_type=MESH,
        )
        copy.start()
        copies.append(copy)
    return copies


def arrive(copies):
    for copy in copies:
        copy.wait_recv()


def forward_exchange(
    mask_ref, heads_ref, outgoing_ref, panels_ref, arrived_ref, near, part, pieces, panel, cut, *sems
):
    here = Place()
    depth, groups = here.depth, here.groups
    pairs = [(sems[2 * k], sems[2 * k + 1]) for k in range(5)]
    each = mask_ref.shape[0] // ACROSS
    per = depth // each
    here.greet()
    heads_out = send_all(
        here.along_x, ACROSS, lambda p, d: heads_ref, lambda d: near.at[d - 1], pairs[0]
    )
    cut_out = send_all(
        here.along_grp, groups, lambda p, d: outgoing_ref.at[p], lambda d: cut.at[here.grp], pairs[1]
    )
    cut[here.grp] = outgoing_ref[here.grp]
    arrive(heads_out)
    for j in range(each):
        section = here.x * each + j
        total = heads_ref[...].astype(F32) * mask_ref[section, here.row]
        for shift in range(1, ACROSS):
            sender = here.z * ACROSS + lax.rem(here.x + ACROSS - shift, ACROSS)
            total += near[shift - 1].astype(F32) * mask_ref[section, sender]
        part[pl.ds(j * per, per)] = total.astype(BF16).reshape(per, HUB // per, -1)
    parts_out = send_all(
        here.along_z, depth, lambda p, d: part.at[p], lambda d: pieces.at[d - 1], pairs[2]
    )
    arrive(parts_out)
    total = part[here.z].astype(F32)
    for shift in range(1, depth):
        total += pieces[shift - 1].astype(F32)
    panel[here.x, here.z] = total.astype(BF16)
    mine = panel.at[here.x, here.z]
    pieces_out = send_all(here.along_z, depth, lambda p, d: mine, lambda d: mine, pairs[3])
    arrive(pieces_out)
    block = panel.at[here.x]
    panels_out = send_all(here.along_x, ACROSS, lambda p, d: block, lambda d: block, pairs[4])
    arrive(cut_out)
    arrived_ref[...] = cut[...]
    arrive(panels_out)
    panels_ref[...] = panel[...]
    for copy in heads_out + cut_out + parts_out + pieces_out + panels_out:
        copy.wait_send()


def backward_exchange(
    mask_ref,
    hub_ref,
    back_ref,
    weight_ref,
    hub_grad_ref,
    returned_ref,
    sum_ref,
    near,
    part,
    pieces,
    whole,
    owned,
    owned_near,
    cut,
    w_near,
    w_part,
    w_pieces,
    w_across,
    w_block,
    w_whole,
    *sems,
):
    here = Place()
    depth, groups = here.depth, here.groups
    pairs = [(sems[2 * k], sems[2 * k + 1]) for k in range(10)]
    each = mask_ref.shape[0] // ACROSS
    per = depth // each
    here.greet()
    sent = []

    def send(*args):
        copies = send_all(*args)
        sent.extend(copies)
        return copies

    hub_out = send(
        here.along_x, ACROSS, lambda p, d: hub_ref.at[p], lambda d: near.at[d - 1], pairs[0]
    )
    weight_out = send(
        here.along_grp, groups, lambda p, d: weight_ref.at[p], lambda d: w_near.at[d - 1], pairs[1]
    )
    cut_out = send(
        here.along_grp, groups, lambda p, d: back_ref.at[p], lambda d: cut.at[here.grp], pairs[2]
    )
    cut[here.grp] = back_ref[here.grp]

    arrive(hub_out)
    total = hub_ref[here.x].astype(F32)
    for shift in range(1, ACROSS):
        total += near[shift - 1].astype(F32)
    part[...] = total.astype(BF16).reshape(part.shape)
    parts_out = send(
        here.along_z, depth, lambda p, d: part.at[p], lambda d: pieces.at[d - 1], pairs[3]
    )

    arrive(weight_out)
    total = weight_ref[here.grp]
    for shift in range(1, groups):
        total += w_near[shift - 1]
    w_part[...] = total.reshape(w_part.shape)
    w_parts_out = send(
        here.along_z, depth, lambda p, d: w_part.at[p], lambda d: w_pieces.at[d - 1], pairs[4]
    )

    arrive(parts_out)
    total = part[here.z].astype(F32)
    for shift in range(1, depth):
        total += pieces[shift - 1].astype(F32)
    whole[here.z] = total.astype(BF16)
    mine = whole.at[here.z]
    whole_out = send(here.along_z, depth, lambda p, d: mine, lambda d: mine, pairs[5])

    arrive(w_parts_out)
    total = w_part[here.z]
    for shift in range(1, depth):
        total += w_pieces[shift - 1]
    w_across[here.x] = total
    w_mine = w_across.at[here.x]
    w_across_out = send(here.along_x, ACROSS, lambda p, d: w_mine, lambda d: w_mine, pairs[6])

    def owned_by(row):
        total = 0.0
        for j in range(each):
            terms = whole[pl.ds(j * per, per)].astype(F32).reshape(HUB, -1)
            total += terms * mask_ref[here.x * each + j, row]
        return total

    arrive(whole_out)
    for shift in range(1, ACROSS):
        peer = here.z * ACROSS + lax.rem(here.x + shift, ACROSS)
        owned[shift - 1] = owned_by(peer).astype(BF16)
    owned_out = send(
        here.along_x, ACROSS, lambda p, d: owned.at[d - 1], lambda d: owned_near.at[d - 1], pairs[7]
    )

    arrive(w_across_out)
    total = w_across[0]
    for k in range(1, ACROSS):
        total += w_across[k]
    w_block[here.z] = total
    w_piece = w_block.at[here.z]
    w_block_out = send(here.along_z, depth, lambda p, d: w_piece, lambda d: w_piece, pairs[8])

    arrive(w_block_out)
    w_whole[here.grp] = w_block[...].reshape(w_whole.shape[1:])
    w_last = w_whole.at[here.grp]
    w_whole_out = send(here.along_grp, groups, lambda p, d: w_last, lambda d: w_last, pairs[9])

    arrive(owned_out)
    total = owned_by(here.row)
    for shift in range(1, ACROSS):
        total += owned_near[shift - 1].astype(F32)
    hub_grad_ref[...] = total
    arrive(cut_out)
    returned_ref[...] = cut[...]
    arrive(w_whole_out)
    sum_ref[...] = w_whole[...]
    for copy in sent:
        copy.wait_send()


def pair_sems(*counts):
    return [pltpu.SemaphoreType.DMA((n - 1,)) for n in counts for _ in range(2)]


def gather_rows(rows_ref, features_ref, out_ref):
    nodes = features_ref.shape[0]
    for start in range(0, out_ref.shape[0], TILE):
        spot = lax.broadcasted_iota(jnp.int32, (TILE, nodes), 1)
        table = jnp.where(spot == rows_ref[start : start + TILE, :], 1.0, 0.0).astype(BF16)
        out_ref[start : start + TILE, :] = dot(table, features_ref[...]).astype(BF16)


def layer_kernel(
    index_ref,
    features_ref,
    cotangent_ref,
    self_ref,
    neighbor_ref,
    values_ref,
    hub_ref,
    panels_ref,
    cut_ref,
    arrived_ref,
    scale_ref,
    hidden_ref,
    total_ref,
    hub_out,
    back_out,
    weight_out,
    acc,
    grads,
    sides,
    hub_acc,
    back_acc,
    self_acc,
    neighbor_acc,
):
    nodes, width = features_ref.shape
    tiles = values_ref.shape[0]
    per = CHUNK // TILE

    def begin(c, carry):
        rows = pl.ds(pl.multiple_of(c * CHUNK, CHUNK), CHUNK)
        acc[rows, :] = dot(hub_ref[rows, :], panels_ref[...]) + dot(
            cut_ref[rows, :], arrived_ref[...]
        )
        return carry

    lax.fori_loop(0, nodes // CHUNK, begin, 0)

    def gather_tile(t, carry):
        rows = pl.ds(pl.multiple_of(index_ref[2 * t] * TILE, TILE), TILE)
        cols = pl.ds(pl.multiple_of(index_ref[2 * t + 1] * TILE, TILE), TILE)
        acc[rows, :] += dot(values_ref[t], features_ref[cols, :])
        return carry

    lax.fori_loop(0, tiles, gather_tile, 0, unroll=4)

    hub_acc[...] = jnp.zeros_like(hub_acc)
    back_acc[...] = jnp.zeros_like(back_acc)
    self_acc[...] = jnp.zeros_like(self_acc)
    neighbor_acc[...] = jnp.zeros_like(neighbor_acc)
    sides[...] = jnp.zeros_like(sides)

    def dense(c, carry):
        rows = pl.ds(pl.multiple_of(c * CHUNK, CHUNK), CHUNK)
        scale = scale_ref[rows, :]
        own = features_ref[rows, :]
        aggregated = (acc[rows, :] * scale).astype(BF16)
        before = dot(own, self_ref[...]) + dot(aggregated, neighbor_ref[...])
        root = 0.7978845608028654
        square = before * before
        bend = jnp.tanh(root * before * (1.0 + 0.044715 * square))
        half = 0.5 * (1.0 + bend)
        hidden_ref[rows, :] = (before * half).astype(BF16)
        slope = half + 0.5 * before * (1.0 - bend * bend) * (
            root * (1.0 + 3.0 * 0.044715 * square)
        )
        grad_before = (cotangent_ref[rows, :].astype(F32) * slope).astype(BF16)
        turned = grad_before.T
        self_acc[...] += dot(turned, own)
        neighbor_acc[...] += dot(turned, aggregated)
        total_ref[rows, :] = dot_cols(grad_before, self_ref[...])
        grad_aggregate = (dot_cols(grad_before, neighbor_ref[...]) * scale).astype(BF16)
        turned = grad_aggregate.T
        for k in range(per):
            grads[c * per + k] = turned[:, k * TILE : (k + 1) * TILE]
        hub_acc[...] += dot(turned, hub_ref[rows, :])
        back_acc[...] += dot(turned, cut_ref[rows, :])
        return carry

    lax.fori_loop(0, nodes // CHUNK, dense, 0)

    def return_tile(t, carry):
        sides[index_ref[2 * t + 1]] += dot(grads[index_ref[2 * t]], values_ref[t])
        return carry

    lax.fori_loop(0, tiles, return_tile, 0, unroll=4)

    def finish(k, carry):
        rows = pl.ds(pl.multiple_of(k * TILE, TILE), TILE)
        total_ref[rows, :] += sides[k].T
        return carry

    lax.fori_loop(0, nodes // TILE, finish, 0)
    hub_out[...] = hub_acc[...].T.astype(BF16)
    back_out[...] = back_acc[...].T.astype(BF16)
    weight_out[:width, :] = self_acc[...].T
    weight_out[width:, :] = neighbor_acc[...].T


def final_kernel(rows_ref, total_ref, hub_ref, returned_ref, out_ref):
    count = rows_ref.shape[1]
    for start in range(0, out_ref.shape[0], CHUNK):
        spot = lax.broadcasted_iota(jnp.int32, (CHUNK, count), 0) + start
        table = jnp.where(spot == rows_ref[...], 1.0, 0.0).astype(BF16)
        total = total_ref[start : start + CHUNK, :] + dot(table, returned_ref[...])
        if start == 0:
            out_ref[:HUB, :] = (total[:HUB] + hub_ref[...]).astype(BF16)
            out_ref[HUB:CHUNK, :] = total[HUB:].astype(BF16)
        else:
            out_ref[start : start + CHUNK, :] = total.astype(BF16)


def shape(dims, dtype):
    return jax.ShapeDtypeStruct(dims, dtype)


def on_device(
    features,
    cotangent,
    self_weight,
    neighbor_weight,
    tile_values,
    tile_index,
    hub_adjacency,
    hub_owner,
    send_rows,
    cut_adjacency,
    degrees,
):
    nodes, width = features.shape
    tiles = nodes // TILE
    groups = lax.axis_size("grp")
    members = lax.axis_size("row")
    depth = members // ACROSS
    sections = hub_owner.shape[1]
    sent = send_rows.shape[2]
    arrivals = groups * sent
    block = sections // ACROSS * HUB
    piece = block // depth
    rows = send_rows[0].reshape(-1)
    mask = (hub_owner[0][:, None] == jnp.arange(members)[None, :]).astype(F32)

    outgoing = pl.pallas_call(
        gather_rows,
        out_shape=shape((arrivals, width), BF16),
        in_specs=[VMEM, VMEM],
        out_specs=VMEM,
        name="gather_rows",
    )(rows[:, None], features)

    panels, arrived = pl.pallas_call(
        forward_exchange,
        out_shape=(
            shape((ACROSS, depth, piece, width), BF16),
            shape((groups, sent, width), BF16),
        ),
        in_specs=[SMEM, VMEM, VMEM],
        out_specs=(VMEM, VMEM),
        scratch_shapes=[
            pltpu.VMEM((ACROSS - 1, HUB, width), BF16),
            pltpu.VMEM((depth, piece, width), BF16),
            pltpu.VMEM((depth - 1, piece, width), BF16),
            pltpu.VMEM((ACROSS, depth, piece, width), BF16),
            pltpu.VMEM((groups, sent, width), BF16),
            *pair_sems(ACROSS, groups, depth, depth, ACROSS),
        ],
        compiler_params=pltpu.CompilerParams(collective_id=0, has_side_effects=True),
        name="forward_exchange",
    )(mask, features[:HUB], outgoing.reshape(groups, sent, width))

    scaling = lax.rsqrt(degrees.astype(F32))[:, None]
    hidden, total, hub_terms, back_rows, weights = pl.pallas_call(
        layer_kernel,
        out_shape=(
            shape((nodes, width), BF16),
            shape((nodes, width), F32),
            shape((sections * HUB, width), BF16),
            shape((arrivals, width), BF16),
            shape((2 * width, width), F32),
        ),
        in_specs=[SMEM] + [VMEM] * 10,
        out_specs=(VMEM,) * 5,
        scratch_shapes=[
            pltpu.VMEM((nodes, width), F32),
            pltpu.VMEM((tiles, width, TILE), BF16),
            pltpu.VMEM((tiles, width, TILE), F32),
            pltpu.VMEM((width, sections * HUB), F32),
            pltpu.VMEM((width, arrivals), F32),
            pltpu.VMEM((width, width), F32),
            pltpu.VMEM((width, width), F32),
        ],
        name="layer",
    )(
        tile_index[0].reshape(-1),
        features,
        cotangent,
        self_weight,
        neighbor_weight,
        tile_values[0],
        hub_adjacency,
        panels.reshape(sections * HUB, width),
        cut_adjacency,
        arrived.reshape(arrivals, width),
        scaling,
    )

    wide = 2 * width // groups
    thin = wide // depth
    hub_grad, returned, weights = pl.pallas_call(
        backward_exchange,
        out_shape=(
            shape((HUB, width), F32),
            shape((groups, sent, width), BF16),
            shape((groups, wide, width), F32),
        ),
        in_specs=[SMEM, VMEM, VMEM, VMEM],
        out_specs=(VMEM,) * 3,
        scratch_shapes=[
            pltpu.VMEM((ACROSS - 1, block, width), BF16),
            pltpu.VMEM((depth, piece, width), BF16),
            pltpu.VMEM((depth - 1, piece, width), BF16),
            pltpu.VMEM((depth, piece, width), BF16),
            pltpu.VMEM((ACROSS - 1, HUB, width), BF16),
            pltpu.VMEM((ACROSS - 1, HUB, width), BF16),
            pltpu.VMEM((groups, sent, width), BF16),
            pltpu.VMEM((groups - 1, wide, width), F32),
            pltpu.VMEM((depth, thin, width), F32),
            pltpu.VMEM((depth - 1, thin, width), F32),
            pltpu.VMEM((ACROSS, thin, width), F32),
            pltpu.VMEM((depth, thin, width), F32),
            pltpu.VMEM((groups, wide, width), F32),
            *pair_sems(
                ACROSS, groups, groups, depth, depth, depth, ACROSS, ACROSS, depth, groups
            ),
        ],
        compiler_params=pltpu.CompilerParams(collective_id=1, has_side_effects=True),
        name="backward_exchange",
    )(
        mask,
        hub_terms.reshape(ACROSS, block, width),
        back_rows.reshape(groups, sent, width),
        weights.reshape(groups, wide, width),
    )

    grad_features = pl.pallas_call(
        final_kernel,
        out_shape=shape((nodes, width), BF16),
        in_specs=[VMEM] * 4,
        out_specs=VMEM,
        name="final",
    )(rows[None, :], total, hub_grad, returned.reshape(arrivals, width))
    weights = weights.reshape(2 * width, width)
    return (hidden, grad_features, weights[:width], weights[width:])


def solution(mesh):
    in_specs = (
        P(("grp", "row"), None),
        P(("grp", "row"), None),
        P(),
        P(),
        P(("grp", "row"), None, None, None),
        P(("grp", "row"), None, None),
        P(("grp", "row"), None),
        P("grp", None),
        P(("grp", "row"), None, None),
        P(("grp", "row"), None),
        P(("grp", "row")),
    )
    out_specs = (P(("grp", "row"), None), P(("grp", "row"), None), P(), P())
    return jax.shard_map(
        on_device, mesh=mesh, in_specs=in_specs, out_specs=out_specs, check_vma=False
    )
```

```python
import jax
import jax.numpy as jnp
from jax import lax
from jax.experimental import pallas as pl
from jax.experimental.pallas import tpu as pltpu
from jax.sharding import PartitionSpec as P

TILE = 128
HUB = 128
ACROSS = 4
CHUNK = 256
F32 = jnp.float32
BF16 = jnp.bfloat16
VMEM = pl.BlockSpec(memory_space=pltpu.VMEM)
SMEM = pl.BlockSpec(memory_space=pltpu.SMEM)
MESH = pl.DeviceIdType.MESH


def dot(left, right):
    return jnp.dot(left, right, preferred_element_type=F32)


def dot_cols(left, right):
    return lax.dot_general(left, right, (((1,), (1,)), ((), ())), preferred_element_type=F32)


class Place:
    def __init__(self):
        self.row = lax.axis_index("row")
        self.grp = lax.axis_index("grp")
        self.groups = lax.axis_size("grp")
        self.depth = lax.axis_size("row") // ACROSS
        self.x = lax.rem(self.row, ACROSS)
        self.z = lax.div(self.row, ACROSS)

    def along_x(self, shift):
        peer = lax.rem(self.x + shift, ACROSS)
        return peer, {"row": self.z * ACROSS + peer}

    def along_z(self, shift):
        peer = lax.rem(self.z + shift, self.depth)
        return peer, {"row": peer * ACROSS + self.x}

    def along_grp(self, shift):
        peer = lax.rem(self.grp + shift, self.groups)
        return peer, {"grp": peer}

    def greet(self):
        barrier = pltpu.get_barrier_semaphore()
        count = 0
        for peers, size in (
            (self.along_x, ACROSS),
            (self.along_z, self.depth),
            (self.along_grp, self.groups),
        ):
            for shift in range(1, size):
                pl.semaphore_signal(
                    barrier, inc=1, device_id=peers(shift)[1], device_id_type=MESH
                )
                count += 1
        pl.semaphore_wait(barrier, count)


def send_all(peers, size, source, target, sems):
    send, recv = sems
    copies = []
    for shift in range(1, size):
        peer, device = peers(shift)
        copy = pltpu.make_async_remote_copy(
            src_ref=source(peer, shift),
            dst_ref=target(shift),
            send_sem=send.at[shift - 1],
            recv_sem=recv.at[shift - 1],
            device_id=device,
            device_id_type=MESH,
        )
        copy.start()
        copies.append(copy)
    return copies


def arrive(copies):
    for copy in copies:
        copy.wait_recv()


def chain_tiles(index_ref, owner_ref, links_ref, mask_ref):
    count = index_ref.shape[1]
    lines = (links_ref.shape[0] - 2 * count) // 2

    for side in range(2):
        base = side * (count + lines)

        def clear(k, carry):
            links_ref[base + count + k] = count
            return carry

        def follow(t, carry):
            line = base + count + index_ref[side, t]
            links_ref[base + t] = links_ref[line]
            links_ref[line] = t
            return carry

        lax.fori_loop(0, lines, clear, 0, unroll=True)
        lax.fori_loop(0, count, follow, 0, unroll=4)

    sections, members = mask_ref.shape

    def blank(k, carry):
        for section in range(sections):
            mask_ref[section, k] = 0.0
        return carry

    lax.fori_loop(0, members, blank, 0, unroll=4)
    for section in range(sections):
        mask_ref[section, owner_ref[0, section]] = 1.0


def sage_kernel(
    index_ref,
    links_ref,
    mask_ref,
    columns_ref,
    degrees_ref,
    self_ref,
    neighbor_ref,
    features_hbm,
    cotangent_hbm,
    values_hbm,
    hub_hbm,
    cut_hbm,
    both_ref,
    sum_ref,
    features_ref,
    cotangent_ref,
    values_ref,
    hub_ref,
    cut_ref,
    scale_ref,
    total_ref,
    slots,
    sides,
    acc,
    grads_before,
    grads,
    table,
    turned_table,
    hub_acc,
    back_acc,
    self_acc,
    neighbor_acc,
    outgoing,
    near,
    part,
    pieces,
    panel,
    arrived,
    hub_terms,
    back_rows,
    b_near,
    b_part,
    b_pieces,
    whole,
    owned,
    owned_near,
    returned,
    weights,
    w_near,
    w_part,
    w_pieces,
    w_across,
    w_block,
    w_whole,
    load_sems,
    *sems,
):
    here = Place()
    depth, groups = here.depth, here.groups
    pairs = [(sems[2 * k], sems[2 * k + 1]) for k in range(len(sems) // 2)]
    lines, _, width = features_ref.shape
    nodes = lines * TILE
    tiles = values_ref.shape[0]
    per_chunk = CHUNK // TILE
    chunks = nodes // CHUNK
    each = mask_ref.shape[0] // ACROSS
    per = depth // each
    sent = []
    loads = []
    for k, (source, target) in enumerate(
        (
            (features_hbm, features_ref),
            (values_hbm, values_ref),
            (cut_hbm, cut_ref),
            (hub_hbm, hub_ref),
            (cotangent_hbm, cotangent_ref),
        )
    ):
        load = pltpu.make_async_copy(source, target, load_sems.at[k])
        load.start()
        loads.append(load)

    def send(*args):
        copies = send_all(*args, pairs[len(sent)])
        sent.append(copies)
        return copies

    def owns(section, row):
        return mask_ref[section, row]

    def chunk_rows(c):
        return pl.ds(pl.multiple_of(c * CHUNK, CHUNK), CHUNK)

    def tile_rows(k):
        return pl.ds(pl.multiple_of(k * TILE, TILE), TILE)

    def own_rows(c):
        return features_ref[pl.ds(c * per_chunk, per_chunk)].reshape(CHUNK, width)

    here.greet()
    heads = features_hbm.at[0]
    heads_out = send(here.along_x, ACROSS, lambda p, d: heads, lambda d: near.at[d - 1])

    loads[0].wait()
    turned_rows = columns_ref[...].T
    count = columns_ref.shape[1]
    for g in range(0, groups, 2):
        picked = jnp.concatenate([turned_rows[:, g : g + 1], turned_rows[:, g + 1 : g + 2]], axis=0)
        spot = lax.broadcasted_iota(jnp.int32, (2 * count, nodes), 1)
        chosen = jnp.where(spot == picked, 1.0, 0.0).astype(BF16)
        table[g * count : (g + 2) * count, :] = chosen
        outgoing[g : g + 2] = dot(chosen, features_ref[...].reshape(nodes, width)).astype(BF16).reshape(2, count, width)
    cut_out = send(
        here.along_grp, groups, lambda p, d: outgoing.at[p], lambda d: arrived.at[here.grp]
    )
    arrived[here.grp] = outgoing[here.grp]

    arrive(heads_out)
    for j in range(each):
        section = here.x * each + j
        total = features_ref[0].astype(F32) * owns(section, here.row)
        for shift in range(1, ACROSS):
            sender = here.z * ACROSS + lax.rem(here.x + ACROSS - shift, ACROSS)
            total += near[shift - 1].astype(F32) * owns(section, sender)
        part[pl.ds(j * per, per)] = total.astype(BF16).reshape(per, HUB // per, width)
    parts_out = send(here.along_z, depth, lambda p, d: part.at[p], lambda d: pieces.at[d - 1])

    loads[1].wait()
    slots[tiles] = jnp.zeros(slots.shape[1:], F32)

    def gather_tile(t, carry):
        slots[t] = slots[links_ref[t]] + dot(values_ref[t], features_ref[index_ref[1, t]])
        return carry

    lax.fori_loop(0, tiles // 2, gather_tile, 0, unroll=4)

    arrive(parts_out)
    total = part[here.z].astype(F32)
    for shift in range(1, depth):
        total += pieces[shift - 1].astype(F32)
    panel[here.x, here.z] = total.astype(BF16)
    mine = panel.at[here.x, here.z]
    pieces_out = send(here.along_z, depth, lambda p, d: mine, lambda d: mine)

    lax.fori_loop(tiles // 2, tiles, gather_tile, 0, unroll=4)

    arrive(pieces_out)
    block = panel.at[here.x]
    panels_out = send(here.along_x, ACROSS, lambda p, d: block, lambda d: block)

    turned_scale = lax.rsqrt(degrees_ref[...].astype(F32)).T
    for k in range(lines):
        scale_ref[k * TILE : (k + 1) * TILE, :] = jnp.broadcast_to(
            turned_scale[:, k : k + 1], (TILE, TILE)
        )
    loads[2].wait()
    arrive(cut_out)

    def begin(c, carry):
        rows = chunk_rows(c)
        total_ref[rows, :] = dot(own_rows(c), self_ref[...])
        inner = dot(cut_ref[rows, :], arrived[...].reshape(-1, width))
        for k in range(per_chunk):
            last = links_ref[tiles + c * per_chunk + k]
            acc[tile_rows(c * per_chunk + k), :] = (
                inner[k * TILE : (k + 1) * TILE] + slots[last]
            )
        return carry

    lax.fori_loop(0, chunks, begin, 0)
    self_acc[...] = jnp.zeros_like(self_acc)
    neighbor_acc[...] = jnp.zeros_like(neighbor_acc)
    hub_acc[...] = jnp.zeros_like(hub_acc)
    back_acc[...] = jnp.zeros_like(back_acc)
    loads[3].wait()
    loads[4].wait()
    arrive(panels_out)

    def spread_scale(rows):
        scale = scale_ref[rows, :]
        return jnp.concatenate([scale] * (width // TILE), axis=1)

    def forward(c, carry):
        rows = chunk_rows(c)
        gathered = acc[rows, :] + dot(hub_ref[rows, :], panel[...].reshape(-1, width))
        aggregated = (gathered * spread_scale(rows)).astype(BF16)
        before = total_ref[rows, :] + dot(aggregated, neighbor_ref[...])
        root = 0.7978845608028654
        square = before * before
        bend = jnp.tanh(root * before * (1.0 + 0.044715 * square))
        half = 0.5 * (1.0 + bend)
        both_ref[0, rows, :] = (before * half).astype(BF16)
        slope = half + 0.5 * before * (1.0 - bend * bend) * (
            root * (1.0 + 3.0 * 0.044715 * square)
        )
        grad_before = (cotangent_ref[rows, :].astype(F32) * slope).astype(BF16)
        grads_before[rows, :] = grad_before
        turned = grad_before.T
        self_acc[...] += dot(turned, own_rows(c))
        neighbor_acc[...] += dot(turned, aggregated)
        return carry

    lax.fori_loop(0, chunks, forward, 0)
    weights[: groups // 2] = self_acc[...].T.reshape(groups // 2, -1, width)
    weights[groups // 2 :] = neighbor_acc[...].T.reshape(groups // 2, -1, width)
    weight_out = send(
        here.along_grp, groups, lambda p, d: weights.at[p], lambda d: w_near.at[d - 1]
    )

    def backward(c, carry):
        rows = chunk_rows(c)
        grad_aggregate = (
            dot_cols(grads_before[rows, :], neighbor_ref[...]) * spread_scale(rows)
        ).astype(BF16)
        turned = grad_aggregate.T
        for k in range(per_chunk):
            grads[c * per_chunk + k] = turned[:, k * TILE : (k + 1) * TILE]
        hub_acc[...] += dot(turned, hub_ref[rows, :])
        back_acc[...] += dot(turned, cut_ref[rows, :])
        return carry

    lax.fori_loop(0, chunks, backward, 0)
    hub_terms[...] = hub_acc[...].T.astype(BF16).reshape(hub_terms.shape)
    hub_out = send(
        here.along_x, ACROSS, lambda p, d: hub_terms.at[p], lambda d: b_near.at[d - 1]
    )
    back_rows[...] = back_acc[...].T.astype(BF16).reshape(back_rows.shape)
    back_out = send(
        here.along_grp, groups, lambda p, d: back_rows.at[p], lambda d: returned.at[here.grp]
    )
    returned[here.grp] = back_rows[here.grp]

    arrive(weight_out)
    total = weights[here.grp]
    for shift in range(1, groups):
        total += w_near[shift - 1]
    w_part[...] = total.reshape(w_part.shape)
    w_parts_out = send(
        here.along_z, depth, lambda p, d: w_part.at[p], lambda d: w_pieces.at[d - 1]
    )

    sides[tiles] = jnp.zeros(sides.shape[1:], F32)
    base = tiles + lines

    def return_tile(t, carry):
        sides[t] = sides[links_ref[base + t]] + dot(grads[index_ref[0, t]], values_ref[t])
        return carry

    lax.fori_loop(0, tiles // 2, return_tile, 0, unroll=4)

    arrive(hub_out)
    total = hub_terms[here.x].astype(F32)
    for shift in range(1, ACROSS):
        total += b_near[shift - 1].astype(F32)
    b_part[...] = total.astype(BF16).reshape(b_part.shape)
    b_parts_out = send(
        here.along_z, depth, lambda p, d: b_part.at[p], lambda d: b_pieces.at[d - 1]
    )

    arrive(w_parts_out)
    total = w_part[here.z]
    for shift in range(1, depth):
        total += w_pieces[shift - 1]
    w_across[here.x] = total
    w_mine = w_across.at[here.x]
    w_across_out = send(here.along_x, ACROSS, lambda p, d: w_mine, lambda d: w_mine)

    lax.fori_loop(tiles // 2, tiles, return_tile, 0, unroll=4)

    arrive(w_across_out)
    total = w_across[0]
    for k in range(1, ACROSS):
        total += w_across[k]
    w_block[here.z] = total
    w_piece = w_block.at[here.z]
    w_block_out = send(here.along_z, depth, lambda p, d: w_piece, lambda d: w_piece)

    arrive(b_parts_out)
    total = b_part[here.z].astype(F32)
    for shift in range(1, depth):
        total += b_pieces[shift - 1].astype(F32)
    whole[here.z] = total.astype(BF16)
    whole_mine = whole.at[here.z]
    whole_out = send(here.along_z, depth, lambda p, d: whole_mine, lambda d: whole_mine)

    def collect(c, carry):
        rows = chunk_rows(c)
        inner = dot_cols(grads_before[rows, :], self_ref[...])
        for k in range(per_chunk):
            last = links_ref[base + tiles + c * per_chunk + k]
            total_ref[tile_rows(c * per_chunk + k), :] = (
                inner[k * TILE : (k + 1) * TILE] + sides[last].T
            )
        turned_table[rows, :] = table[:, rows].T
        return carry

    lax.fori_loop(0, chunks, collect, 0)

    arrive(w_block_out)
    w_whole[here.grp] = w_block[...].reshape(w_whole.shape[1:])
    w_last = w_whole.at[here.grp]
    w_whole_out = send(here.along_grp, groups, lambda p, d: w_last, lambda d: w_last)

    def owned_by(row):
        total = jnp.zeros((HUB, width), F32)
        for j in range(each):
            terms = whole[pl.ds(j * per, per)].astype(F32).reshape(HUB, width)
            total += terms * owns(here.x * each + j, row)
        return total

    arrive(whole_out)
    for shift in range(1, ACROSS):
        peer = here.z * ACROSS + lax.rem(here.x + shift, ACROSS)
        owned[shift - 1] = owned_by(peer).astype(BF16)
    owned_out = send(
        here.along_x, ACROSS, lambda p, d: owned.at[d - 1], lambda d: owned_near.at[d - 1]
    )
    arrive(back_out)

    def scatter(c, carry):
        rows = chunk_rows(c)
        total_ref[rows, :] += dot(turned_table[rows, :], returned[...].reshape(-1, width))
        both_ref[1, rows, :] = total_ref[rows, :].astype(BF16)
        return carry

    lax.fori_loop(0, chunks, scatter, 0)

    arrive(owned_out)
    total = owned_by(here.row)
    for shift in range(1, ACROSS):
        total += owned_near[shift - 1].astype(F32)
    both_ref[1, :HUB, :] = (total_ref[:HUB, :] + total).astype(BF16)
    arrive(w_whole_out)
    sum_ref[...] = w_whole[...]
    for copies in sent:
        for copy in copies:
            copy.wait_send()


def pair_sems(*counts):
    return [pltpu.SemaphoreType.DMA((n - 1,)) for n in counts for _ in range(2)]


def shape(dims, dtype):
    return jax.ShapeDtypeStruct(dims, dtype)


def on_device(
    features,
    cotangent,
    self_weight,
    neighbor_weight,
    tile_values,
    tile_index,
    hub_adjacency,
    hub_owner,
    send_rows,
    cut_adjacency,
    degrees,
):
    nodes, width = features.shape
    lines = nodes // TILE
    tiles = tile_values.shape[1]
    groups = lax.axis_size("grp")
    depth = lax.axis_size("row") // ACROSS
    sections = hub_owner.shape[1]
    sent = send_rows.shape[2]
    arrivals = groups * sent
    block = sections // ACROSS * HUB
    piece = block // depth
    wide = 2 * width // groups
    thin = wide // depth
    index = tile_index[0].T

    links, mask = pl.pallas_call(
        chain_tiles,
        out_shape=(
            shape((2 * (tiles + lines),), jnp.int32),
            shape((sections, lax.axis_size("row")), F32),
        ),
        in_specs=[SMEM, SMEM],
        out_specs=(SMEM, SMEM),
        name="chain_tiles",
    )(index, hub_owner)

    def half(*dims):
        return pltpu.VMEM(dims, BF16)

    def full(*dims):
        return pltpu.VMEM(dims, F32)

    both, weights = pl.pallas_call(
        sage_kernel,
        out_shape=(
            shape((2, nodes, width), BF16),
            shape((groups, wide, width), F32),
        ),
        in_specs=[SMEM] * 3 + [VMEM] * 4 + [pl.BlockSpec(memory_space=pl.ANY)] * 5,
        out_specs=(VMEM,) * 2,
        scratch_shapes=[
            half(lines, TILE, width),
            half(nodes, width),
            half(tiles, TILE, TILE),
            half(nodes, sections * HUB),
            half(nodes, arrivals),
            full(nodes, TILE),
            full(nodes, width),
            full(tiles + 1, TILE, width),
            full(tiles + 1, width, TILE),
            full(nodes, width),
            half(nodes, width),
            half(lines, width, TILE),
            half(arrivals, nodes),
            half(nodes, arrivals),
            full(width, sections * HUB),
            full(width, arrivals),
            full(width, width),
            full(width, width),
            half(groups, sent, width),
            half(ACROSS - 1, HUB, width),
            half(depth, piece, width),
            half(depth - 1, piece, width),
            half(ACROSS, depth, piece, width),
            half(groups, sent, width),
            half(ACROSS, block, width),
            half(groups, sent, width),
            half(ACROSS - 1, block, width),
            half(depth, piece, width),
            half(depth - 1, piece, width),
            half(depth, piece, width),
            half(ACROSS - 1, HUB, width),
            half(ACROSS - 1, HUB, width),
            half(groups, sent, width),
            full(groups, wide, width),
            full(groups - 1, wide, width),
            full(depth, thin, width),
            full(depth - 1, thin, width),
            full(ACROSS, thin, width),
            full(depth, thin, width),
            full(groups, wide, width),
            pltpu.SemaphoreType.DMA((5,)),
            *pair_sems(ACROSS, groups, depth, depth, ACROSS),
            *pair_sems(
                groups, ACROSS, groups, depth, depth, ACROSS, depth, depth, groups, ACROSS
            ),
        ],
        compiler_params=pltpu.CompilerParams(
            collective_id=0, has_side_effects=True, vmem_limit_bytes=60 * 1024 * 1024
        ),
        name="sage",
    )(
        index,
        links,
        mask,
        send_rows[0],
        degrees.reshape(lines, TILE),
        self_weight,
        neighbor_weight,
        features.reshape(lines, TILE, width),
        cotangent,
        tile_values[0],
        hub_adjacency,
        cut_adjacency,
    )
    weights = weights.reshape(2 * width, width)
    return (both[0], both[1], weights[:width], weights[width:])


def solution(mesh):
    in_specs = (
        P(("grp", "row"), None),
        P(("grp", "row"), None),
        P(),
        P(),
        P(("grp", "row"), None, None, None),
        P(("grp", "row"), None, None),
        P(("grp", "row"), None),
        P("grp", None),
        P(("grp", "row"), None, None),
        P(("grp", "row"), None),
        P(("grp", "row")),
    )
    out_specs = (P(("grp", "row"), None), P(("grp", "row"), None), P(), P())
    return jax.shard_map(
        on_device, mesh=mesh, in_specs=in_specs, out_specs=out_specs, check_vma=False
    )
```

```python
import jax
import jax.numpy as jnp
from jax import lax
from jax.experimental import pallas as pl
from jax.experimental.pallas import tpu as pltpu
from jax.sharding import PartitionSpec as P

TILE = 128
HUB = 128
ACROSS = 4
CHUNK = 256
F32 = jnp.float32
BF16 = jnp.bfloat16
VMEM = pl.BlockSpec(memory_space=pltpu.VMEM)
SMEM = pl.BlockSpec(memory_space=pltpu.SMEM)
MESH = pl.DeviceIdType.MESH


def dot(left, right):
    return jnp.dot(left, right, preferred_element_type=F32)


def dot_cols(left, right):
    return lax.dot_general(left, right, (((1,), (1,)), ((), ())), preferred_element_type=F32)


class Place:
    def __init__(self):
        self.row = lax.axis_index("row")
        self.grp = lax.axis_index("grp")
        self.groups = lax.axis_size("grp")
        self.depth = lax.axis_size("row") // ACROSS
        self.x = lax.rem(self.row, ACROSS)
        self.z = lax.div(self.row, ACROSS)

    def along_x(self, shift):
        peer = lax.rem(self.x + shift, ACROSS)
        return peer, {"row": self.z * ACROSS + peer}

    def along_z(self, shift):
        peer = lax.rem(self.z + shift, self.depth)
        return peer, {"row": peer * ACROSS + self.x}

    def along_grp(self, shift):
        peer = lax.rem(self.grp + shift, self.groups)
        return peer, {"grp": peer}

    def greet(self):
        barrier = pltpu.get_barrier_semaphore()
        count = 0
        for peers, size in (
            (self.along_x, ACROSS),
            (self.along_z, self.depth),
            (self.along_grp, self.groups),
        ):
            for shift in range(1, size):
                pl.semaphore_signal(
                    barrier, inc=1, device_id=peers(shift)[1], device_id_type=MESH
                )
                count += 1
        pl.semaphore_wait(barrier, count)


def send_all(peers, size, source, target, sems):
    send, recv = sems
    copies = []
    for shift in range(1, size):
        peer, device = peers(shift)
        copy = pltpu.make_async_remote_copy(
            src_ref=source(peer, shift),
            dst_ref=target(shift),
            send_sem=send.at[shift - 1],
            recv_sem=recv.at[shift - 1],
            device_id=device,
            device_id_type=MESH,
        )
        copy.start()
        copies.append(copy)
    return copies


def arrive(copies):
    for copy in copies:
        copy.wait_recv()


def chain_tiles(index_ref, owner_ref, links_ref, mask_ref):
    count = index_ref.shape[1]
    lines = (links_ref.shape[0] - 2 * count) // 2

    for side in range(2):
        base = side * (count + lines)

        def clear(k, carry):
            links_ref[base + count + k] = count
            return carry

        def follow(t, carry):
            line = base + count + index_ref[side, t]
            links_ref[base + t] = links_ref[line]
            links_ref[line] = t
            return carry

        lax.fori_loop(0, lines, clear, 0, unroll=True)
        lax.fori_loop(0, count, follow, 0, unroll=4)

    sections, members = mask_ref.shape

    def blank(k, carry):
        for section in range(sections):
            mask_ref[section, k] = 0.0
        return carry

    lax.fori_loop(0, members, blank, 0, unroll=4)
    for section in range(sections):
        mask_ref[section, owner_ref[0, section]] = 1.0


def sage_kernel(
    index_ref,
    links_ref,
    mask_ref,
    columns_ref,
    degrees_ref,
    self_ref,
    neighbor_ref,
    features_hbm,
    cotangent_hbm,
    values_hbm,
    hub_hbm,
    cut_hbm,
    both_ref,
    sum_ref,
    features_ref,
    cotangent_ref,
    values_ref,
    hub_ref,
    cut_ref,
    scale_ref,
    total_ref,
    slots,
    sides,
    acc,
    grads_before,
    grads,
    table,
    turned_table,
    hub_acc,
    back_acc,
    self_acc,
    neighbor_acc,
    outgoing,
    near,
    part,
    pieces,
    panel,
    arrived,
    hub_terms,
    back_rows,
    b_near,
    b_part,
    b_pieces,
    whole,
    owned,
    owned_near,
    returned,
    weights,
    w_near,
    w_part,
    w_pieces,
    w_across,
    w_whole,
    load_sems,
    *sems,
):
    here = Place()
    depth, groups = here.depth, here.groups
    pairs = [(sems[2 * k], sems[2 * k + 1]) for k in range(len(sems) // 2)]
    lines, _, width = features_ref.shape
    nodes = lines * TILE
    tiles = values_ref.shape[0]
    per_chunk = CHUNK // TILE
    chunks = nodes // CHUNK
    each = mask_ref.shape[0] // ACROSS
    per = depth // each
    sent = []
    loads = []
    for k, (source, target) in enumerate(
        (
            (features_hbm, features_ref),
            (values_hbm, values_ref),
            (cut_hbm, cut_ref),
            (hub_hbm, hub_ref),
            (cotangent_hbm, cotangent_ref),
        )
    ):
        load = pltpu.make_async_copy(source, target, load_sems.at[k])
        load.start()
        loads.append(load)

    def send(*args):
        copies = send_all(*args, pairs[len(sent)])
        sent.append(copies)
        return copies

    def owns(section, row):
        return mask_ref[section, row]

    def chunk_rows(c):
        return pl.ds(pl.multiple_of(c * CHUNK, CHUNK), CHUNK)

    def tile_rows(k):
        return pl.ds(pl.multiple_of(k * TILE, TILE), TILE)

    def own_rows(c):
        return features_ref[pl.ds(c * per_chunk, per_chunk)].reshape(CHUNK, width)

    here.greet()
    heads = features_hbm.at[0]
    heads_out = send(here.along_x, ACROSS, lambda p, d: heads, lambda d: near.at[d - 1])

    loads[0].wait()
    turned_rows = columns_ref[...].T
    count = columns_ref.shape[1]
    for g in range(0, groups, 2):
        picked = jnp.concatenate([turned_rows[:, g : g + 1], turned_rows[:, g + 1 : g + 2]], axis=0)
        spot = lax.broadcasted_iota(jnp.int32, (2 * count, nodes), 1)
        chosen = jnp.where(spot == picked, 1.0, 0.0).astype(BF16)
        table[g * count : (g + 2) * count, :] = chosen
        outgoing[g : g + 2] = dot(chosen, features_ref[...].reshape(nodes, width)).astype(BF16).reshape(2, count, width)
    cut_out = send(
        here.along_grp, groups, lambda p, d: outgoing.at[p], lambda d: arrived.at[here.grp]
    )
    arrived[here.grp] = outgoing[here.grp]

    arrive(heads_out)
    for j in range(each):
        section = here.x * each + j
        total = features_ref[0].astype(F32) * owns(section, here.row)
        for shift in range(1, ACROSS):
            sender = here.z * ACROSS + lax.rem(here.x + ACROSS - shift, ACROSS)
            total += near[shift - 1].astype(F32) * owns(section, sender)
        part[pl.ds(j * per, per)] = total.astype(BF16).reshape(per, HUB // per, width)
    parts_out = send(here.along_z, depth, lambda p, d: part.at[p], lambda d: pieces.at[d - 1])

    loads[1].wait()
    slots[tiles] = jnp.zeros(slots.shape[1:], F32)

    def gather_tile(t, carry):
        slots[t] = slots[links_ref[t]] + dot(values_ref[t], features_ref[index_ref[1, t]])
        return carry

    lax.fori_loop(0, tiles // 2, gather_tile, 0, unroll=4)

    arrive(parts_out)
    total = part[here.z].astype(F32)
    for shift in range(1, depth):
        total += pieces[shift - 1].astype(F32)
    panel[here.x, here.z] = total.astype(BF16)
    mine = panel.at[here.x, here.z]
    pieces_out = send(here.along_z, depth, lambda p, d: mine, lambda d: mine)
    panels_out = send(here.along_x, ACROSS, lambda p, d: mine, lambda d: mine)

    lax.fori_loop(tiles // 2, tiles, gather_tile, 0, unroll=4)

    for shift in nearest(depth):
        pieces_out[shift - 1].wait_recv()
        piece = panel.at[here.x, lax.rem(here.z + depth - shift, depth)]
        panels_out = panels_out + send(here.along_x, ACROSS, lambda p, d: piece, lambda d: piece)

    turned_scale = lax.rsqrt(degrees_ref[...].astype(F32)).T
    for k in range(lines):
        scale_ref[k * TILE : (k + 1) * TILE, :] = jnp.broadcast_to(
            turned_scale[:, k : k + 1], (TILE, TILE)
        )
    loads[2].wait()
    arrive(cut_out)

    def begin(c, carry):
        rows = chunk_rows(c)
        total_ref[rows, :] = dot(own_rows(c), self_ref[...])
        inner = dot(cut_ref[rows, :], arrived[...].reshape(-1, width))
        for k in range(per_chunk):
            last = links_ref[tiles + c * per_chunk + k]
            acc[tile_rows(c * per_chunk + k), :] = (
                inner[k * TILE : (k + 1) * TILE] + slots[last]
            )
        return carry

    lax.fori_loop(0, chunks, begin, 0)
    self_acc[...] = jnp.zeros_like(self_acc)
    neighbor_acc[...] = jnp.zeros_like(neighbor_acc)
    hub_acc[...] = jnp.zeros_like(hub_acc)
    back_acc[...] = jnp.zeros_like(back_acc)
    loads[3].wait()
    loads[4].wait()
    arrive(panels_out)

    def spread_scale(rows):
        scale = scale_ref[rows, :]
        return jnp.concatenate([scale] * (width // TILE), axis=1)

    def forward(c, carry):
        rows = chunk_rows(c)
        gathered = acc[rows, :] + dot(hub_ref[rows, :], panel[...].reshape(-1, width))
        aggregated = (gathered * spread_scale(rows)).astype(BF16)
        before = total_ref[rows, :] + dot(aggregated, neighbor_ref[...])
        root = 0.7978845608028654
        square = before * before
        bend = jnp.tanh(root * before * (1.0 + 0.044715 * square))
        half = 0.5 * (1.0 + bend)
        both_ref[0, rows, :] = (before * half).astype(BF16)
        slope = half + 0.5 * before * (1.0 - bend * bend) * (
            root * (1.0 + 3.0 * 0.044715 * square)
        )
        grad_before = (cotangent_ref[rows, :].astype(F32) * slope).astype(BF16)
        grads_before[rows, :] = grad_before
        turned = grad_before.T
        self_acc[...] += dot(turned, own_rows(c))
        neighbor_acc[...] += dot(turned, aggregated)
        return carry

    lax.fori_loop(0, chunks, forward, 0)
    weights[: groups // 2] = self_acc[...].T.reshape(groups // 2, -1, width)
    weights[groups // 2 :] = neighbor_acc[...].T.reshape(groups // 2, -1, width)
    weight_out = send(
        here.along_grp, groups, lambda p, d: weights.at[p], lambda d: w_near.at[d - 1]
    )

    def backward(c, carry):
        rows = chunk_rows(c)
        grad_aggregate = (
            dot_cols(grads_before[rows, :], neighbor_ref[...]) * spread_scale(rows)
        ).astype(BF16)
        turned = grad_aggregate.T
        for k in range(per_chunk):
            grads[c * per_chunk + k] = turned[:, k * TILE : (k + 1) * TILE]
        hub_acc[...] += dot(turned, hub_ref[rows, :])
        back_acc[...] += dot(turned, cut_ref[rows, :])
        return carry

    lax.fori_loop(0, chunks, backward, 0)
    hub_terms[...] = hub_acc[...].T.astype(BF16).reshape(hub_terms.shape)
    hub_out = send(
        here.along_x, ACROSS, lambda p, d: hub_terms.at[p], lambda d: b_near.at[d - 1]
    )
    back_rows[...] = back_acc[...].T.astype(BF16).reshape(back_rows.shape)
    back_out = send(
        here.along_grp, groups, lambda p, d: back_rows.at[p], lambda d: returned.at[here.grp]
    )
    returned[here.grp] = back_rows[here.grp]

    arrive(weight_out)
    total = weights[here.grp]
    for shift in range(1, groups):
        total += w_near[shift - 1]
    w_part[...] = total.reshape(w_part.shape)
    w_parts_out = send(
        here.along_z, depth, lambda p, d: w_part.at[p], lambda d: w_pieces.at[d - 1]
    )

    sides[tiles] = jnp.zeros(sides.shape[1:], F32)
    base = tiles + lines

    def return_tile(t, carry):
        sides[t] = sides[links_ref[base + t]] + dot(grads[index_ref[0, t]], values_ref[t])
        return carry

    lax.fori_loop(0, tiles // 2, return_tile, 0, unroll=4)

    arrive(hub_out)
    total = hub_terms[here.x].astype(F32)
    for shift in range(1, ACROSS):
        total += b_near[shift - 1].astype(F32)
    b_part[...] = total.astype(BF16).reshape(b_part.shape)
    b_parts_out = send(
        here.along_z, depth, lambda p, d: b_part.at[p], lambda d: b_pieces.at[d - 1]
    )

    arrive(w_parts_out)
    total = w_part[here.z]
    for shift in range(1, depth):
        total += w_pieces[shift - 1]
    w_across[here.x] = total
    w_mine = w_across.at[here.x]
    w_across_out = send(here.along_x, ACROSS, lambda p, d: w_mine, lambda d: w_mine)

    lax.fori_loop(tiles // 2, tiles, return_tile, 0, unroll=4)

    arrive(w_across_out)
    total = w_across[0]
    for k in range(1, ACROSS):
        total += w_across[k]
    w_whole[here.grp, here.z] = total
    w_own = w_whole.at[here.grp, here.z]
    w_block_out = send(here.along_z, depth, lambda p, d: w_own, lambda d: w_own)
    w_whole_out = send(here.along_grp, groups, lambda p, d: w_own, lambda d: w_own)

    arrive(b_parts_out)
    total = b_part[here.z].astype(F32)
    for shift in range(1, depth):
        total += b_pieces[shift - 1].astype(F32)
    whole[here.z] = total.astype(BF16)
    whole_mine = whole.at[here.z]
    whole_out = send(here.along_z, depth, lambda p, d: whole_mine, lambda d: whole_mine)

    def collect(c, carry):
        rows = chunk_rows(c)
        inner = dot_cols(grads_before[rows, :], self_ref[...])
        for k in range(per_chunk):
            last = links_ref[base + tiles + c * per_chunk + k]
            total_ref[tile_rows(c * per_chunk + k), :] = (
                inner[k * TILE : (k + 1) * TILE] + sides[last].T
            )
        turned_table[rows, :] = table[:, rows].T
        return carry

    lax.fori_loop(0, chunks // 2, collect, 0)

    for shift in nearest(depth):
        w_block_out[shift - 1].wait_recv()
        w_piece = w_whole.at[here.grp, lax.rem(here.z + depth - shift, depth)]
        w_whole_out = w_whole_out + send(
            here.along_grp, groups, lambda p, d: w_piece, lambda d: w_piece
        )

    lax.fori_loop(chunks // 2, chunks, collect, 0)

    def owned_by(row):
        total = jnp.zeros((HUB, width), F32)
        for j in range(each):
            terms = whole[pl.ds(j * per, per)].astype(F32).reshape(HUB, width)
            total += terms * owns(here.x * each + j, row)
        return total

    arrive(whole_out)
    for shift in range(1, ACROSS):
        peer = here.z * ACROSS + lax.rem(here.x + shift, ACROSS)
        owned[shift - 1] = owned_by(peer).astype(BF16)
    owned_out = send(
        here.along_x, ACROSS, lambda p, d: owned.at[d - 1], lambda d: owned_near.at[d - 1]
    )
    arrive(back_out)

    def scatter(c, carry):
        rows = chunk_rows(c)
        total_ref[rows, :] += dot(turned_table[rows, :], returned[...].reshape(-1, width))
        both_ref[1, rows, :] = total_ref[rows, :].astype(BF16)
        return carry

    lax.fori_loop(0, chunks, scatter, 0)

    arrive(owned_out)
    total = owned_by(here.row)
    for shift in range(1, ACROSS):
        total += owned_near[shift - 1].astype(F32)
    both_ref[1, :HUB, :] = (total_ref[:HUB, :] + total).astype(BF16)
    arrive(w_whole_out)
    sum_ref[...] = w_whole[...].reshape(sum_ref.shape)
    for copies in sent:
        for copy in copies:
            copy.wait_send()


def nearest(size):
    return sorted(range(1, size), key=lambda shift: min(shift, size - shift))


def pair_sems(*counts):
    return [pltpu.SemaphoreType.DMA((n - 1,)) for n in counts for _ in range(2)]


def shape(dims, dtype):
    return jax.ShapeDtypeStruct(dims, dtype)


def on_device(
    features,
    cotangent,
    self_weight,
    neighbor_weight,
    tile_values,
    tile_index,
    hub_adjacency,
    hub_owner,
    send_rows,
    cut_adjacency,
    degrees,
):
    nodes, width = features.shape
    lines = nodes // TILE
    tiles = tile_values.shape[1]
    groups = lax.axis_size("grp")
    depth = lax.axis_size("row") // ACROSS
    sections = hub_owner.shape[1]
    sent = send_rows.shape[2]
    arrivals = groups * sent
    block = sections // ACROSS * HUB
    piece = block // depth
    wide = 2 * width // groups
    thin = wide // depth
    index = tile_index[0].T

    links, mask = pl.pallas_call(
        chain_tiles,
        out_shape=(
            shape((2 * (tiles + lines),), jnp.int32),
            shape((sections, lax.axis_size("row")), F32),
        ),
        in_specs=[SMEM, SMEM],
        out_specs=(SMEM, SMEM),
        name="chain_tiles",
    )(index, hub_owner)

    def half(*dims):
        return pltpu.VMEM(dims, BF16)

    def full(*dims):
        return pltpu.VMEM(dims, F32)

    both, weights = pl.pallas_call(
        sage_kernel,
        out_shape=(
            shape((2, nodes, width), BF16),
            shape((groups, wide, width), F32),
        ),
        in_specs=[SMEM] * 3 + [VMEM] * 4 + [pl.BlockSpec(memory_space=pl.ANY)] * 5,
        out_specs=(VMEM,) * 2,
        scratch_shapes=[
            half(lines, TILE, width),
            half(nodes, width),
            half(tiles, TILE, TILE),
            half(nodes, sections * HUB),
            half(nodes, arrivals),
            full(nodes, TILE),
            full(nodes, width),
            full(tiles + 1, TILE, width),
            full(tiles + 1, width, TILE),
            full(nodes, width),
            half(nodes, width),
            half(lines, width, TILE),
            half(arrivals, nodes),
            half(nodes, arrivals),
            full(width, sections * HUB),
            full(width, arrivals),
            full(width, width),
            full(width, width),
            half(groups, sent, width),
            half(ACROSS - 1, HUB, width),
            half(depth, piece, width),
            half(depth - 1, piece, width),
            half(ACROSS, depth, piece, width),
            half(groups, sent, width),
            half(ACROSS, block, width),
            half(groups, sent, width),
            half(ACROSS - 1, block, width),
            half(depth, piece, width),
            half(depth - 1, piece, width),
            half(depth, piece, width),
            half(ACROSS - 1, HUB, width),
            half(ACROSS - 1, HUB, width),
            half(groups, sent, width),
            full(groups, wide, width),
            full(groups - 1, wide, width),
            full(depth, thin, width),
            full(depth - 1, thin, width),
            full(ACROSS, thin, width),
            full(groups, depth, thin, width),
            pltpu.SemaphoreType.DMA((5,)),
            *pair_sems(ACROSS, groups, depth, depth, *[ACROSS] * depth),
            *pair_sems(groups, ACROSS, groups, depth, depth, ACROSS, depth, groups, depth),
            *pair_sems(*[groups] * (depth - 1), ACROSS),
        ],
        compiler_params=pltpu.CompilerParams(
            collective_id=0, has_side_effects=True, vmem_limit_bytes=60 * 1024 * 1024
        ),
        name="sage",
    )(
        index,
        links,
        mask,
        send_rows[0],
        degrees.reshape(lines, TILE),
        self_weight,
        neighbor_weight,
        features.reshape(lines, TILE, width),
        cotangent,
        tile_values[0],
        hub_adjacency,
        cut_adjacency,
    )
    weights = weights.reshape(2 * width, width)
    return (both[0], both[1], weights[:width], weights[width:])


def solution(mesh):
    in_specs = (
        P(("grp", "row"), None),
        P(("grp", "row"), None),
        P(),
        P(),
        P(("grp", "row"), None, None, None),
        P(("grp", "row"), None, None),
        P(("grp", "row"), None),
        P("grp", None),
        P(("grp", "row"), None, None),
        P(("grp", "row"), None),
        P(("grp", "row")),
    )
    out_specs = (P(("grp", "row"), None), P(("grp", "row"), None), P(), P())
    return jax.shard_map(
        on_device, mesh=mesh, in_specs=in_specs, out_specs=out_specs, check_vma=False
    )
```
